32 devices in a mesh: dp: 2 (over y), tm: 8 (over z, core), height: 2 (over x).
Axes of the slice: x: 2, y: 2, z: 4, core: 2. Of those that a mesh axis runs over, the one named last changes fastest.
Arguments:
- clip_input: bfloat16 [2, 32, 8, 96, 128], P('dp', 'tm', 'height'), may hold values from -6 to 6
- cotangent: bfloat16 [2, 32, 8, 96, 128], P('dp', 'tm', 'height'), may hold values from -6 to 6
- first_kernel: bfloat16 [2592, 96], replicated, may hold values from -0.125 to 0.125
- second_kernel: bfloat16 [2592, 96], replicated, may hold values from -0.125 to 0.125
Outputs:
- block_output: float32 [2, 32, 8, 96, 128], P('dp', 'tm', 'height')
- input_grad: float32 [2, 32, 8, 96, 128], P('dp', 'tm', 'height')
- first_grad: float32 [2592, 96], P('dp')
- second_grad: float32 [2592, 96], P('dp')
The draws below stay inside these ranges and needn't reach their ends.
All inputs are finite; a program needn't handle non-finite values.
Results may differ from the reference program's by a relative error of at most 0.0048.
Values may be sent and summed in bfloat16 or wider, within the bound.
A program may use at most 64 MiB of HBM per device.

```python
import math
import jax
import jax.numpy as jnp
from jax import lax

C = 96
COLS = 128
CLIPS = 2
FRAMES = 32
ROWS = 8


def shard_levels(rng, shape, pieces, least, largest):
    loudness, own = 1.0, jax.random.fold_in(rng, 6)
    for dim, blocks in pieces:
        heights = jnp.exp(jax.random.uniform(jax.random.fold_in(own, dim), (blocks,), jnp.float32, least / len(pieces), largest / len(pieces)))
        loudness = loudness * jnp.repeat(heights, shape[dim] // blocks).reshape([-1 if axis == dim else 1 for axis in range(len(shape))])
    return loudness


def normal_values(stream_key, shape, width, reach, split=(), kind=jnp.bfloat16):
    values = jax.random.normal(stream_key, shape, jnp.float32) * width
    if len(split) > 0:
        values = shard_levels(stream_key, shape, split, -0.22, 0.18) * values
    return jnp.clip(values, min=-reach, max=reach).astype(kind)


def setup_inputs(seed: int = 0) -> dict:
    seeds = jax.random.split(jax.random.key(seed), 5)
    clip_input = normal_values(seeds[0], (CLIPS, FRAMES, ROWS, C, COLS), 1.0, 6.0, ((0, 2), (1, 8), (2, 2)))
    cotangent = normal_values(seeds[1], (CLIPS, FRAMES, ROWS, C, COLS), 1.0, 6.0, ((0, 2), (1, 8), (2, 2)))
    first_kernel = normal_values(seeds[2], (27 * C, C), (27 * C) ** -0.5, 0.125)
    second_kernel = normal_values(seeds[3], (27 * C, C), (27 * C) ** -0.5, 0.125)
    return dict(clip_input=clip_input, cotangent=cotangent, first_kernel=first_kernel, second_kernel=second_kernel)


EPSILON = 1e-06

def norm_silu(field):
    factor = lax.rsqrt(lax.optimization_barrier(jnp.mean(field * field, axis=2, keepdims=True)) + EPSILON)
    return jax.nn.silu(field * factor)

def conv_clip(field, kernel):
    channels = field.shape[2]
    left_side = jnp.transpose(field, (2, 0, 1, 3))[None]
    right_side = jnp.transpose(kernel.reshape(3, 3, 3, channels, channels), (4, 3, 0, 1, 2))
    result = lax.conv_general_dilated(left_side, right_side, (1, 1, 1), ((2, 0), (1, 1), (1, 1)), precision=lax.Precision.HIGHEST)
    return jnp.transpose(result[0], (1, 2, 0, 3))

def to_bf16_and_back(value):
    return lax.optimization_barrier(value.astype(jnp.bfloat16)).astype(jnp.float32)

def reference(clip_input, cotangent, first_kernel, second_kernel):
    kernel_one = first_kernel.astype(jnp.float32)
    kernel_two = second_kernel.astype(jnp.float32)

    def one_clip(paired):
        source = paired[0].astype(jnp.float32)
        upstream = paired[1].astype(jnp.float32)
        first_act = to_bf16_and_back(norm_silu(source))
        middle = conv_clip(first_act, kernel_one)
        second_act = to_bf16_and_back(norm_silu(middle))
        branch = conv_clip(second_act, kernel_two)
        block_output = source + branch
        unused, pull_two = jax.vjp(conv_clip, second_act, kernel_two)
        second_back, second_term = pull_two(upstream)
        unused, pull_mid = jax.vjp(norm_silu, middle)
        middle_grad = to_bf16_and_back(pull_mid(second_back)[0])
        unused, pull_one = jax.vjp(conv_clip, first_act, kernel_one)
        first_back, first_term = pull_one(middle_grad)
        unused, pull_src = jax.vjp(norm_silu, source)
        input_grad = upstream + pull_src(first_back)[0]
        return (block_output, input_grad, first_term, second_term)
    outputs, grads_in, first_terms, second_terms = lax.map(one_clip, (clip_input, cotangent))
    factor = 1.0 / math.sqrt(CLIPS * FRAMES * ROWS * COLS)
    first_grad = lax.optimization_barrier(jnp.sum(first_terms, axis=0)) * factor
    second_grad = lax.optimization_barrier(jnp.sum(second_terms, axis=0)) * factor
    return (outputs, grads_in, first_grad, second_grad)
```

```python
import functools
import math

import jax
import jax.numpy as jnp
from jax import lax
from jax.experimental import pallas as pl
from jax.experimental.pallas import tpu as pltpu
from jax.sharding import PartitionSpec as P

EPSILON = 1e-06
MESH_IDS = pl.DeviceIdType.MESH


def factor_of(value):
    return lax.rsqrt(jnp.mean(value * value, axis=0, keepdims=True) + EPSILON)


def act(value):
    scaled = value * factor_of(value)
    return scaled / (1.0 + jnp.exp(-scaled))


def act_back(value, grad):
    factor = factor_of(value)
    scaled = value * factor
    gate = 1.0 / (1.0 + jnp.exp(-scaled))
    inner = grad * (gate * (1.0 + scaled * (1.0 - gate)))
    return factor * (inner - scaled * jnp.mean(inner * scaled, axis=0, keepdims=True))


def body(
    sizes,
    scale,
    x,
    cot,
    turned_one,
    turned_two,
    block_out,
    input_out,
    grad_one,
    grad_two,
    x_own,
    cot_own,
    turned,
    ahead_weights,
    back_weights,
    acts_one,
    acts_two,
    grads_two,
    grads_one,
    middle,
    second_act,
    middle_grad,
    partial,
    block_own,
    input_own,
    grad_own,
    time_halo,
    row_halo,
    corner_halo,
    terms,
    swap_out,
    swap_in,
    wide,
    narrow,
    plane_in,
    wide_half,
    narrow_half,
    half_in,
    wide_z,
    narrow_z,
    got_z,
    mine,
    halo_send,
    halo_recv,
    send,
    recv,
    local_sem,
):
    dp, heights, depth = sizes
    frames, rows, channels, cols = x.shape
    shards = 2 * depth
    chunk = grad_one.shape[1]
    band, width = narrow_z.shape[2:]
    shard = lax.axis_index("tm")
    core, level = shard % 2, shard // 2
    clip, half = lax.axis_index("dp"), lax.axis_index("height")
    other = 1 - half
    has_before, has_after = shard > 0, shard < shards - 1
    edge_row = (rows - 1) * other
    halo_row = (rows + 1) * other
    rim_row = (rows + 1) * half

    barrier = pltpu.get_barrier_semaphore()
    partner = {"tm": level * 2 + 1 - core}
    clip_peers = [(clip + step) % dp for step in range(1, dp)]
    level_peers = [(level + step) % depth for step in range(1, depth)]
    places = [partner, {"height": other}]
    places += [{"dp": peer} for peer in clip_peers]
    places += [{"tm": peer * 2 + core} for peer in level_peers]

    def greet(place):
        pl.semaphore_signal(barrier, inc=1, device_id=place, device_id_type=MESH_IDS)

    for place in places:
        greet(place)

    outer = shard + 2 * core - 1
    has_outer = jnp.logical_and(outer >= 0, outer < shards)

    @pl.when(has_outer)
    def _():
        greet({"tm": outer})

    @pl.when(has_before)
    def _():
        greet({"tm": shard - 1, "height": other})

    @pl.when(has_after)
    def _():
        greet({"tm": shard + 1, "height": other})

    taken = [0]

    def bring(source, target):
        copy = pltpu.make_async_copy(source, target, local_sem.at[taken[0]])
        taken[0] += 1
        copy.start()
        return copy

    inner = pl.ds(2, frames)
    weights_come = [bring(turned_one, turned.at[0]), bring(turned_two, turned.at[1])]
    x_comes = bring(x, x_own)
    cot_comes = bring(cot, cot_own.at[inner])

    near = has_outer.astype(jnp.int32) + has_before.astype(jnp.int32) + has_after.astype(jnp.int32)
    pl.semaphore_wait(barrier, len(places) + near)

    def remote(source, target, sender, receiver, place):
        return pltpu.make_async_remote_copy(
            src_ref=source,
            dst_ref=target,
            send_sem=sender,
            recv_sem=receiver,
            device_id=place,
            device_id_type=MESH_IDS,
        )

    def exchange(own, slot, ahead):
        step = -1 if ahead else 1
        start = 0 if ahead else frames - 2
        goes, comes = (has_before, has_after) if ahead else (has_after, has_before)
        span = pl.ds(start, 2)
        along = remote(own.at[span], time_halo.at[slot], halo_send.at[slot, 0], halo_recv.at[slot, 0], {"tm": shard + step})
        across = remote(own.at[:, edge_row], row_halo.at[slot], halo_send.at[slot, 1], halo_recv.at[slot, 1], {"height": other})
        corner = remote(
            own.at[span, edge_row],
            corner_halo.at[slot],
            halo_send.at[slot, 2],
            halo_recv.at[slot, 2],
            {"tm": shard + step, "height": other},
        )

        def send_time():
            @pl.when(goes)
            def _():
                along.start()
                corner.start()

        def wait_time():
            @pl.when(goes)
            def _():
                along.wait_send()
                corner.wait_send()

            @pl.when(comes)
            def _():
                along.wait_recv()
                corner.wait_recv()

        return across.start, send_time, across.wait, wait_time

    x_rows_go, x_time_goes, x_rows, x_time = exchange(x, 0, False)
    cot_rows_go, cot_time_goes, cot_rows, cot_time = exchange(cot, 1, True)
    x_rows_go()
    x_time_goes()
    cot_rows_go()
    cot_time_goes()

    lane = lax.broadcasted_iota(jnp.int32, (channels, cols), 1)

    def place_tile(field, frame, row, value):
        wide_value = value.astype(jnp.float32)
        left = jnp.where(lane == 0, 0.0, pltpu.roll(wide_value, 1, axis=1))
        right = jnp.where(lane == cols - 1, 0.0, pltpu.roll(wide_value, cols - 1, axis=1))
        field[frame, row, 0:channels] = left.astype(jnp.bfloat16)
        field[frame, row, channels : 2 * channels] = value
        field[frame, row, 2 * channels : 3 * channels] = right.astype(jnp.bfloat16)

    def clear(field, ahead):
        outside = frames if ahead else 0
        blank = jnp.zeros((3 * channels, cols), jnp.bfloat16)
        for frame in range(frames + 2):
            field[frame, rim_row] = blank
        for frame in range(outside, outside + 2):
            for row in range(rows + 2):
                field[frame, row] = blank

    def fill_rows(field, slot, ahead, make):
        inside = 0 if ahead else 2
        for frame in range(frames):
            place_tile(field, inside + frame, halo_row, make(row_halo[slot, frame]))

    def fill_time(field, slot, ahead, make):
        outside = frames if ahead else 0

        @pl.when(has_after if ahead else has_before)
        def _():
            def step(frame, carry):
                for row in range(rows):
                    place_tile(field, outside + frame, row + 1, make(time_halo[slot, frame, row]))
                place_tile(field, outside + frame, halo_row, make(corner_halo[slot, frame]))
                return carry

            lax.fori_loop(0, 2, step, 0)

    def conv(field, weights, order, finish):
        seen = [0] * frames

        def step(frame):
            taps = [tap for tap in range(3) if 0 <= frame - tap < frames]
            least = taps[0]
            patch = jnp.concatenate([field[frame, row : row + 3].reshape(9 * channels, cols) for row in range(rows)], axis=1)
            lines = weights[least * channels : (taps[-1] + 1) * channels]
            part = jnp.dot(lines, patch, preferred_element_type=jnp.float32)
            for tap in taps:
                target = frame - tap
                seen[target] += 1
                for row in range(rows):
                    value = part[(tap - least) * channels : (tap - least + 1) * channels, row * cols : (row + 1) * cols]
                    if seen[target] > 1:
                        value = partial[target, row] + value
                    if seen[target] == 3:
                        finish(target, row, value)
                    else:
                        partial[target, row] = value

        return [functools.partial(step, frame) for frame in order]

    def run(steps):
        for step in steps:
            step()

    def kernel_grad(slot, field, grad):
        tiles = [(frame, row) for frame in range(frames + 2) for row in range(rows)]
        left = jnp.concatenate(
            [jnp.concatenate([grad[frame - tap + 2, row] for frame, row in tiles], axis=1) for tap in range(3)], axis=0
        )
        right = jnp.concatenate([field[frame, row : row + 3].reshape(9 * channels, cols) for frame, row in tiles], axis=1)
        found = lax.dot_general(left, right, (((1,), (1,)), ((), ())), preferred_element_type=jnp.float32)
        span = 9 * channels
        for tap in range(3):
            for piece in range(dp):
                start, stop = max(tap * span, piece * chunk), min((tap + 1) * span, (piece + 1) * chunk)
                if start < stop:
                    value = found[tap * channels : (tap + 1) * channels, start - tap * span : stop - tap * span]
                    terms[slot, piece, :, start - piece * chunk : stop - piece * chunk] = value

    def as_act(value):
        return act(value.astype(jnp.float32)).astype(jnp.bfloat16)

    def same(value):
        return value

    for field, ahead in ((acts_one, False), (acts_two, False), (grads_two, True), (grads_one, True)):
        clear(field, ahead)
    blank_tile = jnp.zeros((channels, cols), jnp.bfloat16)
    for padded in (cot_own, middle_grad):
        for frame in (0, 1, frames + 2, frames + 3):
            for row in range(rows):
                padded[frame, row] = blank_tile

    x_comes.wait()

    def own_acts(frame, carry):
        for row in range(rows):
            place_tile(acts_one, frame + 2, row + 1, as_act(x_own[frame, row]))
        return carry

    lax.fori_loop(0, frames, own_acts, 0)
    for index, copy in enumerate(weights_come):
        copy.wait()
        plain = jnp.transpose(turned[index])
        for tap in range(3):
            lines = slice(tap * channels, (tap + 1) * channels)
            ahead_weights[index, lines] = turned[index, :, tap * 9 * channels : (tap + 1) * 9 * channels]
            last = 26 - 9 * tap
            tiles = [plain[(last - place) * channels : (last - place + 1) * channels] for place in range(9)]
            back_weights[index, lines] = jnp.concatenate(tiles, axis=1)
    cot_comes.wait()

    def own_grads(frame, carry):
        for row in range(rows):
            place_tile(grads_two, frame, row + 1, cot_own[frame + 2, row])
        return carry

    lax.fori_loop(0, frames, own_grads, 0)

    def finish_middle(frame, row, value):
        middle[frame, row] = value
        rounded = act(value).astype(jnp.bfloat16)
        second_act[frame, row] = rounded
        place_tile(acts_two, frame + 2, row + 1, rounded)

    act_rows_go, act_time_goes, act_rows, act_time = exchange(second_act, 2, False)
    x_rows()
    fill_rows(acts_one, 0, False, as_act)
    steps = conv(acts_one, ahead_weights[0], range(frames + 1, -1, -1), finish_middle)
    run(steps[:frames])
    act_time_goes()
    x_time()
    fill_time(acts_one, 0, False, as_act)
    run(steps[frames:])
    act_rows_go()

    def finish_back(frame, row, value):
        rounded = act_back(middle[frame, row], value).astype(jnp.bfloat16)
        middle_grad[frame + 2, row] = rounded
        place_tile(grads_one, frame, row + 1, rounded)

    grad_rows_go, grad_time_goes, grad_rows, grad_time = exchange(middle_grad.at[inner], 3, True)
    cot_rows()
    fill_rows(grads_two, 1, True, same)
    steps = conv(grads_two, back_weights[1], range(frames + 2), finish_back)
    run(steps[:frames])
    grad_time_goes()
    cot_time()
    fill_time(grads_two, 1, True, same)
    run(steps[frames:])
    grad_rows_go()

    used = [0]

    def send_to(source, target, place):
        slot = used[0]
        used[0] += 1
        copy = remote(source, target, send.at[slot], recv.at[slot], place)
        copy.start()
        return copy

    def wait_all(copies):
        for copy in copies:
            copy.wait()

    def reduce(index, plane_first):
        share = channels // 2

        def piece_of(piece, line, owner):
            lines = pl.ds(pl.multiple_of(owner * share + line * band, band), band)
            return terms[index, piece, lines]

        for piece in range(dp):
            for line in range(2):
                value = piece_of(piece, line, 1 - core).astype(jnp.bfloat16)
                for block in range(depth):
                    swap_out[index, piece, line, block] = value[:, block * width : (block + 1) * width]
        swap = send_to(swap_out.at[index], swap_in.at[index], partner)
        yield
        swap.wait()
        for piece in range(dp):
            for line in range(2):
                value = piece_of(piece, line, core)
                for block in range(depth):
                    summed = value[:, block * width : (block + 1) * width]
                    summed = summed + swap_in[index, piece, line, block].astype(jnp.float32)
                    wide[index, piece, line, block] = summed
                    narrow[index, piece, line, block] = summed.astype(jnp.bfloat16)
        if plane_first:
            copies = [
                send_to(narrow.at[index, peer], plane_in.at[index, i], {"dp": peer}) for i, peer in enumerate(clip_peers)
            ]
            yield
            wait_all(copies)
            summed = wide[index, clip]
            for i in range(dp - 1):
                summed = summed + plane_in[index, i].astype(jnp.float32)
            wide_half[index, 0:2] = summed
            narrow_half[index, 0:2] = summed.astype(jnp.bfloat16)
            copy = send_to(narrow_half.at[index, other], half_in.at[index, 0], {"height": other})
            yield
            copy.wait()
            summed = wide_half[index, half] + half_in[index, 0].astype(jnp.float32)
        else:
            copies = [
                send_to(narrow.at[index, piece, other], half_in.at[index, piece], {"height": other}) for piece in range(dp)
            ]
            yield
            wait_all(copies)
            for piece in range(dp):
                summed = wide[index, piece, half] + half_in[index, piece].astype(jnp.float32)
                wide_half[index, piece] = summed
                narrow_half[index, piece] = summed.astype(jnp.bfloat16)
            copies = [
                send_to(narrow_half.at[index, peer], plane_in.at[index, i, 0], {"dp": peer})
                for i, peer in enumerate(clip_peers)
            ]
            yield
            wait_all(copies)
            summed = wide_half[index, clip]
            for i in range(dp - 1):
                summed = summed + plane_in[index, i, 0].astype(jnp.float32)
        wide_z[index] = summed
        narrow_z[index] = summed.astype(jnp.bfloat16)
        copies = [
            send_to(narrow_z.at[index, peer], got_z.at[index, i], {"tm": peer * 2 + core})
            for i, peer in enumerate(level_peers)
        ]
        yield
        wait_all(copies)
        summed = wide_z[index, level]
        for i in range(depth - 1):
            summed = summed + got_z[index, i].astype(jnp.float32)
        mine[index, core, half, level] = summed.astype(jnp.bfloat16)
        own = mine.at[index, core, half, level]
        copies = [send_to(own, own, {"tm": peer * 2 + core}) for peer in level_peers]
        yield
        wait_all(copies)
        own = mine.at[index, core, half]
        copy = send_to(own, own, {"height": other})
        yield
        copy.wait()
        own = mine.at[index, core]
        copy = send_to(own, own, partner)
        yield
        copy.wait()
        for place in range(2):
            for line in range(2):
                top = place * share + line * band
                for block in range(depth):
                    start, stop = block * width, min((block + 1) * width, chunk)
                    if start < stop:
                        value = mine[index, place, line, block].astype(jnp.float32) * scale
                        grad_own[index, top : top + band, start:stop] = value[:, : stop - start]
        copies_out.append(bring(grad_own.at[index], (grad_one, grad_two)[index]))

    copies_out = []

    def finish_branch(frame, row, value):
        block_own[frame, row] = x_own[frame, row].astype(jnp.float32) + value
        if row == rows - 1:
            copies_out.append(bring(block_own.at[frame], block_out.at[frame]))

    def finish_input(frame, row, value):
        back = act_back(x_own[frame, row].astype(jnp.float32), value)
        input_own[frame, row] = cot_own[frame + 2, row].astype(jnp.float32) + back
        if row == rows - 1:
            copies_out.append(bring(input_own.at[frame], input_out.at[frame]))

    kernel_grad(0, acts_one, middle_grad)
    first = reduce(0, True)
    next(first)
    act_rows()
    fill_rows(acts_two, 2, False, same)
    act_time()
    fill_time(acts_two, 2, False, same)
    kernel_grad(1, acts_two, cot_own)
    next(first)
    second = reduce(1, False)
    next(second)
    steps = conv(acts_two, ahead_weights[1], range(frames + 2), finish_branch)
    run(steps[:3])
    next(second)
    run(steps[3:])
    next(first)
    grad_rows()
    fill_rows(grads_one, 3, True, same)
    grad_time()
    fill_time(grads_one, 3, True, same)
    steps = conv(grads_one, back_weights[0], range(frames + 2), finish_input)
    run(steps[:2])
    next(second)
    run(steps[2:4])
    next(first)
    run(steps[4:])
    next(second)
    going = [first, second]
    while going:
        for task in list(going):
            if next(task, 0) == 0:
                going.remove(task)
    wait_all(copies_out)


def local(clip_input, cotangent, first_kernel, second_kernel):
    dp, heights, depth = (lax.axis_size("dp"), lax.axis_size("height"), lax.axis_size("tm") // 2)
    assert heights == 2
    _, frames, rows, channels, cols = clip_input.shape
    taps = first_kernel.shape[0]
    chunk = taps // dp
    band = channels // 4
    width = -(-chunk // (cols * depth)) * cols
    sends = 2 * (1 + (dp - 1) + max(1, dp) + 2 * (depth - 1) + 2)
    tile = (channels, cols)
    own = (frames, rows) + tile
    block = (depth, band, width)
    anywhere = pl.BlockSpec(memory_space=pl.ANY)
    field = pltpu.VMEM((frames + 2, rows + 2, 3 * channels, cols), jnp.bfloat16)
    padded = pltpu.VMEM((frames + 4, rows) + tile, jnp.bfloat16)
    weights = pltpu.VMEM((2, 3 * channels, 9 * channels), jnp.bfloat16)
    positions = frames * rows * cols * dp * heights * lax.axis_size("tm")
    block_output, input_grad, grad_one, grad_two = pl.pallas_call(
        functools.partial(body, (dp, heights, depth), 1.0 / math.sqrt(positions)),
        out_shape=(
            jax.ShapeDtypeStruct(own, jnp.float32),
            jax.ShapeDtypeStruct(own, jnp.float32),
            jax.ShapeDtypeStruct((channels, chunk), jnp.float32),
            jax.ShapeDtypeStruct((channels, chunk), jnp.float32),
        ),
        in_specs=[anywhere] * 4,
        out_specs=(anywhere,) * 4,
        scratch_shapes=[
            pltpu.VMEM(own, jnp.bfloat16),
            padded,
            pltpu.VMEM((2, channels, taps), jnp.bfloat16),
            weights,
            weights,
            field,
            field,
            field,
            field,
            pltpu.VMEM(own, jnp.float32),
            pltpu.VMEM(own, jnp.bfloat16),
            padded,
            pltpu.VMEM(own, jnp.float32),
            pltpu.VMEM(own, jnp.float32),
            pltpu.VMEM(own, jnp.float32),
            pltpu.VMEM((2, channels, chunk), jnp.float32),
            pltpu.VMEM((4, 2, rows) + tile, jnp.bfloat16),
            pltpu.VMEM((4, frames) + tile, jnp.bfloat16),
            pltpu.VMEM((4, 2) + tile, jnp.bfloat16),
            pltpu.VMEM((2, dp, channels, depth * width), jnp.float32),
            pltpu.VMEM((2, dp, 2) + block, jnp.bfloat16),
            pltpu.VMEM((2, dp, 2) + block, jnp.bfloat16),
            pltpu.VMEM((2, dp, 2) + block, jnp.float32),
            pltpu.VMEM((2, dp, 2) + block, jnp.bfloat16),
            pltpu.VMEM((2, dp - 1, 2) + block, jnp.bfloat16),
            pltpu.VMEM((2, max(2, dp)) + block, jnp.float32),
            pltpu.VMEM((2, max(2, dp)) + block, jnp.bfloat16),
            pltpu.VMEM((2, dp) + block, jnp.bfloat16),
            pltpu.VMEM((2,) + block, jnp.float32),
            pltpu.VMEM((2,) + block, jnp.bfloat16),
            pltpu.VMEM((2, depth - 1, band, width), jnp.bfloat16),
            pltpu.VMEM((2, 2, 2) + block, jnp.bfloat16),
            pltpu.SemaphoreType.DMA((4, 3)),
            pltpu.SemaphoreType.DMA((4, 3)),
            pltpu.SemaphoreType.DMA((sends,)),
            pltpu.SemaphoreType.DMA((sends,)),
            pltpu.SemaphoreType.DMA((6 + 2 * frames,)),
        ],
        compiler_params=pltpu.CompilerParams(collective_id=0, has_side_effects=True),
        name="block_step",
    )(clip_input[0], cotangent[0], first_kernel.T, second_kernel.T)
    return (block_output[None], input_grad[None], grad_one.T, grad_two.T)


def solution(mesh):
    split = P("dp", "tm", "height", None, None)
    return jax.shard_map(
        local,
        mesh=mesh,
        in_specs=(split, split, P(), P()),
        out_specs=(split, split, P("dp", None), P("dp", None)),
        check_vma=False,
    )
```

```python
import functools
import math

import jax
import jax.numpy as jnp
from jax import lax
from jax.experimental import pallas as pl
from jax.experimental.pallas import tpu as pltpu
from jax.sharding import PartitionSpec as P

EPSILON = 1e-06
MESH_IDS = pl.DeviceIdType.MESH
VMEM_BYTES = 40 << 20


def factor_of(value):
    return lax.rsqrt(jnp.mean(value * value, axis=0, keepdims=True) + EPSILON)


def act(value):
    scaled = value * factor_of(value)
    return scaled / (1.0 + jnp.exp(-scaled))


def act_back(value, grad):
    factor = factor_of(value)
    scaled = value * factor
    gate = 1.0 / (1.0 + jnp.exp(-scaled))
    inner = grad * (gate * (1.0 + scaled * (1.0 - gate)))
    return factor * (inner - scaled * jnp.mean(inner * scaled, axis=0, keepdims=True))


def body(
    sizes,
    scale,
    x,
    cot,
    turned_one,
    turned_two,
    block_out,
    input_out,
    grad_one,
    grad_two,
    x_own,
    cot_own,
    turned,
    ahead_weights,
    back_weights,
    acts_one,
    acts_two,
    grads_two,
    grads_one,
    middle,
    second_act,
    middle_grad,
    partial,
    block_own,
    input_own,
    grad_own,
    time_halo,
    row_halo,
    corner_halo,
    terms,
    swap_out,
    swap_in,
    wide,
    narrow,
    plane_in,
    wide_z,
    narrow_z,
    got_z,
    mine,
    halo_send,
    halo_recv,
    send,
    recv,
    local_sem,
):
    dp, heights, depth = sizes
    frames, rows, channels, cols = x.shape
    shards = 2 * depth
    chunk = grad_one.shape[1]
    band, width = narrow_z.shape[2:]
    shard = lax.axis_index("tm")
    core, level = shard % 2, shard // 2
    clip, half = lax.axis_index("dp"), lax.axis_index("height")
    other = 1 - half
    has_before, has_after = shard > 0, shard < shards - 1
    edge_row = (rows - 1) * other
    halo_row = (rows + 1) * other
    rim_row = (rows + 1) * half

    barrier = pltpu.get_barrier_semaphore()
    partner = {"tm": level * 2 + 1 - core}
    clip_peers = [(clip + step) % dp for step in range(1, dp)]
    level_peers = [(level + step) % depth for step in range(1, depth)]
    places = [partner, {"height": other}]
    places += [{"dp": peer} for peer in clip_peers]
    places += [{"tm": peer * 2 + core} for peer in level_peers]

    plane_peers = [(peer, owner) for owner in (half, other) for peer in clip_peers] + [(clip, other)]
    places += [{"dp": peer, "height": other} for peer in clip_peers]

    def greet(place):
        pl.semaphore_signal(barrier, inc=1, device_id=place, device_id_type=MESH_IDS)

    for place in places:
        greet(place)

    outer = shard + 2 * core - 1
    has_outer = jnp.logical_and(outer >= 0, outer < shards)

    @pl.when(has_outer)
    def _():
        greet({"tm": outer})

    @pl.when(has_before)
    def _():
        greet({"tm": shard - 1, "height": other})

    @pl.when(has_after)
    def _():
        greet({"tm": shard + 1, "height": other})

    taken = [0]

    def bring(source, target):
        copy = pltpu.make_async_copy(source, target, local_sem.at[taken[0]])
        taken[0] += 1
        copy.start()
        return copy

    inner = pl.ds(2, frames)
    weights_come = [bring(turned_one, turned.at[0]), bring(turned_two, turned.at[1])]
    x_comes = bring(x, x_own)
    cot_comes = bring(cot, cot_own.at[inner])

    near = has_outer.astype(jnp.int32) + has_before.astype(jnp.int32) + has_after.astype(jnp.int32)
    pl.semaphore_wait(barrier, len(places) + near)

    def remote(source, target, sender, receiver, place):
        return pltpu.make_async_remote_copy(
            src_ref=source,
            dst_ref=target,
            send_sem=sender,
            recv_sem=receiver,
            device_id=place,
            device_id_type=MESH_IDS,
        )

    def exchange(own, slot, ahead):
        step = -1 if ahead else 1
        start = 0 if ahead else frames - 2
        goes, comes = (has_before, has_after) if ahead else (has_after, has_before)
        span = pl.ds(start, 2)
        along = remote(own.at[span], time_halo.at[slot], halo_send.at[slot, 0], halo_recv.at[slot, 0], {"tm": shard + step})
        across = remote(own.at[:, edge_row], row_halo.at[slot], halo_send.at[slot, 1], halo_recv.at[slot, 1], {"height": other})
        corner = remote(
            own.at[span, edge_row],
            corner_halo.at[slot],
            halo_send.at[slot, 2],
            halo_recv.at[slot, 2],
            {"tm": shard + step, "height": other},
        )

        def send_time():
            @pl.when(goes)
            def _():
                along.start()
                corner.start()

        def wait_time():
            @pl.when(goes)
            def _():
                along.wait_send()
                corner.wait_send()

            @pl.when(comes)
            def _():
                along.wait_recv()
                corner.wait_recv()

        return across.start, send_time, across.wait, wait_time

    x_rows_go, x_time_goes, x_rows, x_time = exchange(x, 0, False)
    cot_rows_go, cot_time_goes, cot_rows, cot_time = exchange(cot, 1, True)
    x_rows_go()
    x_time_goes()
    cot_rows_go()
    cot_time_goes()

    lane = lax.broadcasted_iota(jnp.int32, (channels, cols), 1)

    def place_tile(field, frame, row, value):
        wide_value = value.astype(jnp.float32)
        left = jnp.where(lane == 0, 0.0, pltpu.roll(wide_value, 1, axis=1))
        right = jnp.where(lane == cols - 1, 0.0, pltpu.roll(wide_value, cols - 1, axis=1))
        field[frame, row, 0:channels] = left.astype(jnp.bfloat16)
        field[frame, row, channels : 2 * channels] = value
        field[frame, row, 2 * channels : 3 * channels] = right.astype(jnp.bfloat16)

    def clear(field, ahead):
        outside = frames if ahead else 0
        blank = jnp.zeros((3 * channels, cols), jnp.bfloat16)
        for frame in range(frames + 2):
            field[frame, rim_row] = blank
        for frame in range(outside, outside + 2):
            for row in range(rows + 2):
                field[frame, row] = blank

    def fill_rows(field, slot, ahead, make):
        inside = 0 if ahead else 2
        for frame in range(frames):
            place_tile(field, inside + frame, halo_row, make(row_halo[slot, frame]))

    def fill_time(field, slot, ahead, make):
        outside = frames if ahead else 0

        @pl.when(has_after if ahead else has_before)
        def _():
            def step(frame, carry):
                for row in range(rows):
                    place_tile(field, outside + frame, row + 1, make(time_halo[slot, frame, row]))
                place_tile(field, outside + frame, halo_row, make(corner_halo[slot, frame]))
                return carry

            lax.fori_loop(0, 2, step, 0)

    def conv(field, weights, order, finish):
        seen = [0] * frames

        def step(frame):
            taps = [tap for tap in range(3) if 0 <= frame - tap < frames]
            least = taps[0]
            patch = jnp.concatenate([field[frame, row : row + 3].reshape(9 * channels, cols) for row in range(rows)], axis=1)
            lines = weights[least * channels : (taps[-1] + 1) * channels]
            part = jnp.dot(lines, patch, preferred_element_type=jnp.float32)
            for tap in taps:
                target = frame - tap
                seen[target] += 1
                for row in range(rows):
                    value = part[(tap - least) * channels : (tap - least + 1) * channels, row * cols : (row + 1) * cols]
                    if seen[target] > 1:
                        value = partial[target, row] + value
                    if seen[target] == 3:
                        finish(target, row, value)
                    else:
                        partial[target, row] = value

        return [functools.partial(step, frame) for frame in order]

    def run(steps):
        for step in steps:
            step()

    def kernel_grad(slot, field, grad):
        tiles = [(frame, row) for frame in range(frames + 2) for row in range(rows)]
        left = jnp.concatenate(
            [jnp.concatenate([grad[frame - tap + 2, row] for frame, row in tiles], axis=1) for tap in range(3)], axis=0
        )
        right = jnp.concatenate([field[frame, row : row + 3].reshape(9 * channels, cols) for frame, row in tiles], axis=1)
        found = lax.dot_general(left, right, (((1,), (1,)), ((), ())), preferred_element_type=jnp.float32)
        span = 9 * channels
        for tap in range(3):
            for piece in range(dp):
                start, stop = max(tap * span, piece * chunk), min((tap + 1) * span, (piece + 1) * chunk)
                if start < stop:
                    value = found[tap * channels : (tap + 1) * channels, start - tap * span : stop - tap * span]
                    terms[slot, piece, :, start - piece * chunk : stop - piece * chunk] = value

    def as_act(value):
        return act(value.astype(jnp.float32)).astype(jnp.bfloat16)

    def same(value):
        return value

    for field, ahead in ((acts_one, False), (acts_two, False), (grads_two, True), (grads_one, True)):
        clear(field, ahead)
    blank_tile = jnp.zeros((channels, cols), jnp.bfloat16)
    for padded in (cot_own, middle_grad):
        for frame in (0, 1, frames + 2, frames + 3):
            for row in range(rows):
                padded[frame, row] = blank_tile

    x_comes.wait()

    def own_acts(frame, carry):
        for row in range(rows):
            place_tile(acts_one, frame + 2, row + 1, as_act(x_own[frame, row]))
        return carry

    lax.fori_loop(0, frames, own_acts, 0)
    for index, copy in enumerate(weights_come):
        copy.wait()
        plain = jnp.transpose(turned[index])
        for tap in range(3):
            lines = slice(tap * channels, (tap + 1) * channels)
            ahead_weights[index, lines] = turned[index, :, tap * 9 * channels : (tap + 1) * 9 * channels]
            last = 26 - 9 * tap
            tiles = [plain[(last - place) * channels : (last - place + 1) * channels] for place in range(9)]
            back_weights[index, lines] = jnp.concatenate(tiles, axis=1)
    cot_comes.wait()

    def own_grads(frame, carry):
        for row in range(rows):
            place_tile(grads_two, frame, row + 1, cot_own[frame + 2, row])
        return carry

    lax.fori_loop(0, frames, own_grads, 0)

    def finish_middle(frame, row, value):
        middle[frame, row] = value
        rounded = act(value).astype(jnp.bfloat16)
        second_act[frame, row] = rounded
        place_tile(acts_two, frame + 2, row + 1, rounded)

    act_rows_go, act_time_goes, act_rows, act_time = exchange(second_act, 2, False)
    x_rows()
    fill_rows(acts_one, 0, False, as_act)
    steps = conv(acts_one, ahead_weights[0], range(frames + 1, -1, -1), finish_middle)
    run(steps[:frames])
    act_time_goes()
    x_time()
    fill_time(acts_one, 0, False, as_act)
    run(steps[frames:])
    act_rows_go()

    def finish_back(frame, row, value):
        rounded = act_back(middle[frame, row], value).astype(jnp.bfloat16)
        middle_grad[frame + 2, row] = rounded
        place_tile(grads_one, frame, row + 1, rounded)

    grad_rows_go, grad_time_goes, grad_rows, grad_time = exchange(middle_grad.at[inner], 3, True)
    cot_rows()
    fill_rows(grads_two, 1, True, same)
    steps = conv(grads_two, back_weights[1], range(frames + 2), finish_back)
    run(steps[:frames])
    grad_time_goes()
    cot_time()
    fill_time(grads_two, 1, True, same)
    run(steps[frames:])
    grad_rows_go()

    used = [0]

    def send_to(source, target, place):
        slot = used[0]
        used[0] += 1
        copy = remote(source, target, send.at[slot], recv.at[slot], place)
        copy.start()
        return copy

    def wait_all(copies):
        for copy in copies:
            copy.wait()

    def reduce(index):
        share = channels // 2

        def lines_of(owner, line):
            return pl.ds(pl.multiple_of(owner * share + line * band, band), band)

        for piece in range(dp):
            for line in range(2):
                swap_out[index, piece, line] = terms[index, piece, lines_of(1 - core, line)].astype(jnp.bfloat16)
        swap = send_to(swap_out.at[index], swap_in.at[index], partner)
        yield
        swap.wait()
        for piece in range(dp):
            for line in range(2):
                summed = terms[index, piece, lines_of(core, line)] + swap_in[index, piece, line].astype(jnp.float32)
                wide[index, piece, line] = summed
                narrow[index, piece, line] = summed.astype(jnp.bfloat16)
        copies = [
            send_to(narrow.at[index, places[0], places[1]], plane_in.at[index, i], {"dp": places[0], "height": places[1]})
            for i, places in enumerate(plane_peers)
        ]
        yield
        wait_all(copies)
        summed = wide[index, clip, half]
        for i in range(len(plane_peers)):
            summed = summed + plane_in[index, i].astype(jnp.float32)
        for block in range(depth):
            start, stop = block * width, min((block + 1) * width, summed.shape[1])
            if start < stop:
                value = summed[:, start:stop]
                wide_z[index, block, :, : stop - start] = value
                narrow_z[index, block, :, : stop - start] = value.astype(jnp.bfloat16)
        copies = [
            send_to(narrow_z.at[index, peer], got_z.at[index, i], {"tm": peer * 2 + core})
            for i, peer in enumerate(level_peers)
        ]
        yield
        wait_all(copies)
        summed = wide_z[index, level]
        for i in range(depth - 1):
            summed = summed + got_z[index, i].astype(jnp.float32)
        mine[index, core, half, level] = summed.astype(jnp.bfloat16)
        own = mine.at[index, core, half, level]
        along = [send_to(own, own, {"tm": peer * 2 + core}) for peer in level_peers]
        across, inside = [], []

        def pass_on(owner, step, targets):
            block = mine.at[index, core, owner, (level + depth - step) % depth]
            for copies, place in targets:
                copies.append(send_to(block, block, place))

        both = ((across, {"height": other}), (inside, partner))
        pass_on(half, 0, both)
        yield
        for step in range(1, depth):
            along[step - 1].wait()
            pass_on(half, step, both)
        yield
        for step in range(depth):
            across[step].wait()
            pass_on(other, step, both[1:])
        yield
        wait_all(inside)
        for place in range(2):
            for line in range(2):
                top = place * share + line * band
                for block in range(depth):
                    start, stop = block * width, min((block + 1) * width, chunk)
                    if start < stop:
                        value = mine[index, place, line, block].astype(jnp.float32) * scale
                        grad_own[index, top : top + band, start:stop] = value[:, : stop - start]
        copies_out.append(bring(grad_own.at[index], (grad_one, grad_two)[index]))

    copies_out = []

    def finish_branch(frame, row, value):
        block_own[frame, row] = x_own[frame, row].astype(jnp.float32) + value
        if row == rows - 1:
            copies_out.append(bring(block_own.at[frame], block_out.at[frame]))

    def finish_input(frame, row, value):
        back = act_back(x_own[frame, row].astype(jnp.float32), value)
        input_own[frame, row] = cot_own[frame + 2, row].astype(jnp.float32) + back
        if row == rows - 1:
            copies_out.append(bring(input_own.at[frame], input_out.at[frame]))

    kernel_grad(0, acts_one, middle_grad)
    first = reduce(0)
    next(first)
    act_rows()
    fill_rows(acts_two, 2, False, same)
    act_time()
    fill_time(acts_two, 2, False, same)
    kernel_grad(1, acts_two, cot_own)
    next(first)
    second = reduce(1)
    next(second)
    steps = conv(acts_two, ahead_weights[1], range(frames + 2), finish_branch)
    run(steps[:3])
    next(second)
    run(steps[3:])
    grad_rows()
    fill_rows(grads_one, 3, True, same)
    grad_time()
    fill_time(grads_one, 3, True, same)
    next(first)
    steps = conv(grads_one, back_weights[0], range(frames + 2), finish_input)
    run(steps[:3])
    next(second)
    run(steps[3:])
    going = [first, second]
    while going:
        for task in list(going):
            if next(task, 0) == 0:
                going.remove(task)
    wait_all(copies_out)


def deliver(*refs):
    count = len(refs) // 2
    copies = [pltpu.make_async_copy(refs[i], refs[count + i], refs[-1].at[i]) for i in range(count)]
    for copy in copies:
        copy.start()
    for copy in copies:
        copy.wait()


def local(clip_input, cotangent, first_kernel, second_kernel):
    dp, heights, depth = (lax.axis_size("dp"), lax.axis_size("height"), lax.axis_size("tm") // 2)
    assert heights == 2
    _, frames, rows, channels, cols = clip_input.shape
    taps = first_kernel.shape[0]
    chunk = taps // dp
    band = channels // 4
    width = -(-chunk // (cols * depth)) * cols
    lanes = -(-chunk // cols) * cols
    sends = 2 * (1 + (2 * dp - 1) + 2 * (depth - 1) + 3 * depth)
    tile = (channels, cols)
    own = (frames, rows) + tile
    block = (depth, band, width)
    anywhere = pl.BlockSpec(memory_space=pl.ANY)
    field = pltpu.VMEM((frames + 2, rows + 2, 3 * channels, cols), jnp.bfloat16)
    padded = pltpu.VMEM((frames + 4, rows) + tile, jnp.bfloat16)
    weights = pltpu.VMEM((2, 3 * channels, 9 * channels), jnp.bfloat16)
    positions = frames * rows * cols * dp * heights * lax.axis_size("tm")
    found = pl.pallas_call(
        functools.partial(body, (dp, heights, depth), 1.0 / math.sqrt(positions)),
        out_shape=(
            jax.ShapeDtypeStruct(own, jnp.float32),
            jax.ShapeDtypeStruct(own, jnp.float32),
            jax.ShapeDtypeStruct((channels, chunk), jnp.float32),
            jax.ShapeDtypeStruct((channels, chunk), jnp.float32),
        ),
        in_specs=[pl.BlockSpec(memory_space=pltpu.HBM)] * 4,
        out_specs=(anywhere,) * 4,
        scratch_shapes=[
            pltpu.VMEM(own, jnp.bfloat16),
            padded,
            pltpu.VMEM((2, channels, taps), jnp.bfloat16),
            weights,
            weights,
            field,
            field,
            field,
            field,
            pltpu.VMEM(own, jnp.float32),
            pltpu.VMEM(own, jnp.bfloat16),
            padded,
            pltpu.VMEM(own, jnp.float32),
            pltpu.VMEM(own, jnp.float32),
            pltpu.VMEM(own, jnp.float32),
            pltpu.VMEM((2, channels, chunk), jnp.float32),
            pltpu.VMEM((4, 2, rows) + tile, jnp.bfloat16),
            pltpu.VMEM((4, frames) + tile, jnp.bfloat16),
            pltpu.VMEM((4, 2) + tile, jnp.bfloat16),
            pltpu.VMEM((2, dp, channels, lanes), jnp.float32),
            pltpu.VMEM((2, dp, 2, band, lanes), jnp.bfloat16),
            pltpu.VMEM((2, dp, 2, band, lanes), jnp.bfloat16),
            pltpu.VMEM((2, dp, 2, band, lanes), jnp.float32),
            pltpu.VMEM((2, dp, 2, band, lanes), jnp.bfloat16),
            pltpu.VMEM((2, 2 * dp - 1, band, lanes), jnp.bfloat16),
            pltpu.VMEM((2,) + block, jnp.float32),
            pltpu.VMEM((2,) + block, jnp.bfloat16),
            pltpu.VMEM((2, depth - 1, band, width), jnp.bfloat16),
            pltpu.VMEM((2, 2, 2) + block, jnp.bfloat16),
            pltpu.SemaphoreType.DMA((4, 3)),
            pltpu.SemaphoreType.DMA((4, 3)),
            pltpu.SemaphoreType.DMA((sends,)),
            pltpu.SemaphoreType.DMA((sends,)),
            pltpu.SemaphoreType.DMA((6 + 2 * frames,)),
        ],
        compiler_params=pltpu.CompilerParams(
            collective_id=0, has_side_effects=True, vmem_limit_bytes=VMEM_BYTES
        ),
        name="block_step",
    )(*[pltpu.with_memory_space_constraint(value, pltpu.HBM) for value in (clip_input[0], cotangent[0], first_kernel.T, second_kernel.T)])
    block_output, input_grad, grad_one, grad_two = pl.pallas_call(
        deliver,
        out_shape=[jax.ShapeDtypeStruct(value.shape, value.dtype) for value in found],
        in_specs=[anywhere] * len(found),
        out_specs=[anywhere] * len(found),
        scratch_shapes=[pltpu.SemaphoreType.DMA((len(found),))],
        compiler_params=pltpu.CompilerParams(vmem_limit_bytes=1 << 20),
        name="deliver",
    )(*found)
    return (block_output[None], input_grad[None], grad_one.T, grad_two.T)


def solution(mesh):
    split = P("dp", "tm", "height", None, None)
    return jax.shard_map(
        local,
        mesh=mesh,
        in_specs=(split, split, P(), P()),
        out_specs=(split, split, P("dp", None), P("dp", None)),
        check_vma=False,
    )
```

```python
import functools
import math

import jax
import jax.numpy as jnp
from jax import lax
from jax.experimental import pallas as pl
from jax.experimental.pallas import tpu as pltpu
from jax.sharding import PartitionSpec as P

EPSILON = 1e-06
MESH_IDS = pl.DeviceIdType.MESH
VMEM_BYTES = 40 << 20


def factor_of(value):
    return lax.rsqrt(jnp.mean(value * value, axis=0, keepdims=True) + EPSILON)


def act(value):
    scaled = value * factor_of(value)
    return scaled / (1.0 + jnp.exp(-scaled))


def act_back(value, grad):
    factor = factor_of(value)
    scaled = value * factor
    gate = 1.0 / (1.0 + jnp.exp(-scaled))
    inner = grad * (gate * (1.0 + scaled * (1.0 - gate)))
    return factor * (inner - scaled * jnp.mean(inner * scaled, axis=0, keepdims=True))


def body(
    sizes,
    scale,
    x,
    cot,
    turned_one,
    turned_two,
    block_out,
    input_out,
    grad_one,
    grad_two,
    x_own,
    cot_own,
    turned,
    ahead_weights,
    back_weights,
    acts_one,
    acts_two,
    grads_two,
    grads_one,
    middle,
    second_act,
    middle_grad,
    partial,
    block_own,
    input_own,
    grad_own,
    time_halo,
    row_halo,
    corner_halo,
    terms,
    swap_out,
    swap_in,
    wide,
    narrow,
    plane_in,
    wide_z,
    narrow_z,
    got_z,
    mine,
    halo_send,
    halo_recv,
    send,
    recv,
    local_sem,
):
    dp, heights, depth = sizes
    frames, rows, channels, cols = x.shape
    shards = 2 * depth
    chunk = grad_one.shape[1]
    band, width = narrow_z.shape[2:]
    shard = lax.axis_index("tm")
    core, level = shard % 2, shard // 2
    clip, half = lax.axis_index("dp"), lax.axis_index("height")
    other = 1 - half
    has_before, has_after = shard > 0, shard < shards - 1
    edge_row = (rows - 1) * other
    halo_row = (rows + 1) * other
    rim_row = (rows + 1) * half

    barrier = pltpu.get_barrier_semaphore()
    partner = {"tm": level * 2 + 1 - core}
    clip_peers = [(clip + step) % dp for step in range(1, dp)]
    level_peers = [(level + step) % depth for step in range(1, depth)]
    places = [partner, {"height": other}]
    places += [{"dp": peer} for peer in clip_peers]
    places += [{"tm": peer * 2 + core} for peer in level_peers]

    plane_peers = [(peer, owner) for owner in (half, other) for peer in clip_peers] + [(clip, other)]
    places += [{"dp": peer, "height": other} for peer in clip_peers]

    def greet(place):
        pl.semaphore_signal(barrier, inc=1, device_id=place, device_id_type=MESH_IDS)

    for place in places:
        greet(place)

    outer = shard + 2 * core - 1
    has_outer = jnp.logical_and(outer >= 0, outer < shards)

    @pl.when(has_outer)
    def _():
        greet({"tm": outer})

    @pl.when(has_before)
    def _():
        greet({"tm": shard - 1, "height": other})

    @pl.when(has_after)
    def _():
        greet({"tm": shard + 1, "height": other})

    taken = [0]

    def bring(source, target):
        copy = pltpu.make_async_copy(source, target, local_sem.at[taken[0]])
        taken[0] += 1
        copy.start()
        return copy

    inner = pl.ds(2, frames)
    weights_come = [bring(turned_one, turned.at[0]), bring(turned_two, turned.at[1])]
    x_comes = bring(x, x_own)
    cot_comes = bring(cot, cot_own.at[inner])

    near = has_outer.astype(jnp.int32) + has_before.astype(jnp.int32) + has_after.astype(jnp.int32)
    pl.semaphore_wait(barrier, len(places) + near)

    def remote(source, target, sender, receiver, place):
        return pltpu.make_async_remote_copy(
            src_ref=source,
            dst_ref=target,
            send_sem=sender,
            recv_sem=receiver,
            device_id=place,
            device_id_type=MESH_IDS,
        )

    def exchange(own, slot, ahead):
        step = -1 if ahead else 1
        start = 0 if ahead else frames - 2
        goes, comes = (has_before, has_after) if ahead else (has_after, has_before)
        span = pl.ds(start, 2)
        along = remote(own.at[span], time_halo.at[slot], halo_send.at[slot, 0], halo_recv.at[slot, 0], {"tm": shard + step})
        across = remote(own.at[:, edge_row], row_halo.at[slot], halo_send.at[slot, 1], halo_recv.at[slot, 1], {"height": other})
        corner = remote(
            own.at[span, edge_row],
            corner_halo.at[slot],
            halo_send.at[slot, 2],
            halo_recv.at[slot, 2],
            {"tm": shard + step, "height": other},
        )

        def send_time():
            @pl.when(goes)
            def _():
                along.start()
                corner.start()

        def wait_time():
            @pl.when(goes)
            def _():
                along.wait_send()
                corner.wait_send()

            @pl.when(comes)
            def _():
                along.wait_recv()
                corner.wait_recv()

        return across.start, send_time, across.wait, wait_time

    x_rows_go, x_time_goes, x_rows, x_time = exchange(x, 0, False)
    cot_rows_go, cot_time_goes, cot_rows, cot_time = exchange(cot, 1, True)
    x_rows_go()
    x_time_goes()

    lane = lax.broadcasted_iota(jnp.int32, (channels, cols), 1)

    def place_tile(field, frame, row, value):
        wide_value = value.astype(jnp.float32)
        left = jnp.where(lane == 0, 0.0, pltpu.roll(wide_value, 1, axis=1))
        right = jnp.where(lane == cols - 1, 0.0, pltpu.roll(wide_value, cols - 1, axis=1))
        field[frame, row, 0:channels] = left.astype(jnp.bfloat16)
        field[frame, row, channels : 2 * channels] = value
        field[frame, row, 2 * channels : 3 * channels] = right.astype(jnp.bfloat16)

    def clear(field, ahead):
        outside = frames if ahead else 0
        blank = jnp.zeros((3 * channels, cols), jnp.bfloat16)
        for frame in range(frames + 2):
            field[frame, rim_row] = blank
        for frame in range(outside, outside + 2):
            for row in range(rows + 2):
                field[frame, row] = blank

    def fill_rows(field, slot, ahead, make):
        inside = 0 if ahead else 2
        for frame in range(frames):
            place_tile(field, inside + frame, halo_row, make(row_halo[slot, frame]))

    def fill_time(field, slot, ahead, make):
        outside = frames if ahead else 0

        @pl.when(has_after if ahead else has_before)
        def _():
            def step(frame, carry):
                for row in range(rows):
                    place_tile(field, outside + frame, row + 1, make(time_halo[slot, frame, row]))
                place_tile(field, outside + frame, halo_row, make(corner_halo[slot, frame]))
                return carry

            lax.fori_loop(0, 2, step, 0)

    def conv(field, weights, order, finish):
        seen = [0] * frames

        def step(frame):
            taps = [tap for tap in range(3) if 0 <= frame - tap < frames]
            least = taps[0]
            patch = jnp.concatenate([field[frame, row : row + 3].reshape(9 * channels, cols) for row in range(rows)], axis=1)
            lines = weights[least * channels : (taps[-1] + 1) * channels]
            part = jnp.dot(lines, patch, preferred_element_type=jnp.float32)
            for tap in taps:
                target = frame - tap
                seen[target] += 1
                for row in range(rows):
                    value = part[(tap - least) * channels : (tap - least + 1) * channels, row * cols : (row + 1) * cols]
                    if seen[target] > 1:
                        value = partial[target, row] + value
                    if seen[target] == 3:
                        finish(target, row, value)
                    else:
                        partial[target, row] = value

        return [functools.partial(step, frame) for frame in order]

    def run(steps):
        for step in steps:
            step()

    def kernel_grad(slot, field, grad):
        tiles = [(frame, row) for frame in range(frames + 2) for row in range(rows)]
        left = jnp.concatenate(
            [jnp.concatenate([grad[frame - tap + 2, row] for frame, row in tiles], axis=1) for tap in range(3)], axis=0
        )
        right = jnp.concatenate([field[frame, row : row + 3].reshape(9 * channels, cols) for frame, row in tiles], axis=1)
        found = lax.dot_general(left, right, (((1,), (1,)), ((), ())), preferred_element_type=jnp.float32)
        span = 9 * channels
        for tap in range(3):
            for piece in range(dp):
                start, stop = max(tap * span, piece * chunk), min((tap + 1) * span, (piece + 1) * chunk)
                if start < stop:
                    value = found[tap * channels : (tap + 1) * channels, start - tap * span : stop - tap * span]
                    terms[slot, piece, :, start - piece * chunk : stop - piece * chunk] = value

    def as_act(value):
        return act(value.astype(jnp.float32)).astype(jnp.bfloat16)

    def same(value):
        return value

    for field, ahead in ((acts_one, False), (acts_two, False), (grads_two, True), (grads_one, True)):
        clear(field, ahead)
    blank_tile = jnp.zeros((channels, cols), jnp.bfloat16)
    for padded in (cot_own, middle_grad):
        for frame in (0, 1, frames + 2, frames + 3):
            for row in range(rows):
                padded[frame, row] = blank_tile

    x_comes.wait()

    def own_acts(frame, carry):
        for row in range(rows):
            place_tile(acts_one, frame + 2, row + 1, as_act(x_own[frame, row]))
        return carry

    lax.fori_loop(0, frames, own_acts, 0)
    for index, copy in enumerate(weights_come):
        copy.wait()
        plain = jnp.transpose(turned[index])
        for tap in range(3):
            lines = slice(tap * channels, (tap + 1) * channels)
            ahead_weights[index, lines] = turned[index, :, tap * 9 * channels : (tap + 1) * 9 * channels]
            last = 26 - 9 * tap
            tiles = [plain[(last - place) * channels : (last - place + 1) * channels] for place in range(9)]
            back_weights[index, lines] = jnp.concatenate(tiles, axis=1)
    cot_comes.wait()

    def own_grads(frame, carry):
        for row in range(rows):
            place_tile(grads_two, frame, row + 1, cot_own[frame + 2, row])
        return carry

    lax.fori_loop(0, frames, own_grads, 0)

    def finish_middle(frame, row, value):
        middle[frame, row] = value
        rounded = act(value).astype(jnp.bfloat16)
        second_act[frame, row] = rounded
        place_tile(acts_two, frame + 2, row + 1, rounded)

    act_rows_go, act_time_goes, act_rows, act_time = exchange(second_act, 2, False)
    cot_rows_go()
    cot_time_goes()
    x_rows()
    fill_rows(acts_one, 0, False, as_act)
    steps = conv(acts_one, ahead_weights[0], range(frames + 1, -1, -1), finish_middle)
    run(steps[:frames])
    act_time_goes()
    x_time()
    fill_time(acts_one, 0, False, as_act)
    run(steps[frames:])
    act_rows_go()

    def finish_back(frame, row, value):
        rounded = act_back(middle[frame, row], value).astype(jnp.bfloat16)
        middle_grad[frame + 2, row] = rounded
        place_tile(grads_one, frame, row + 1, rounded)

    grad_rows_go, grad_time_goes, grad_rows, grad_time = exchange(middle_grad.at[inner], 3, True)
    cot_rows()
    fill_rows(grads_two, 1, True, same)
    steps = conv(grads_two, back_weights[1], range(frames + 2), finish_back)
    run(steps[:frames])
    grad_time_goes()
    cot_time()
    fill_time(grads_two, 1, True, same)
    run(steps[frames:])
    grad_rows_go()

    used = [0]

    def send_to(source, target, place):
        slot = used[0]
        used[0] += 1
        copy = remote(source, target, send.at[slot], recv.at[slot], place)
        copy.start()
        return copy

    def wait_all(copies):
        for copy in copies:
            copy.wait()

    def reduce(index):
        share = channels // 2

        def lines_of(owner, line):
            return pl.ds(pl.multiple_of(owner * share + line * band, band), band)

        for piece in range(dp):
            for line in range(2):
                swap_out[index, piece, line] = terms[index, piece, lines_of(1 - core, line)].astype(jnp.bfloat16)
        swap = send_to(swap_out.at[index], swap_in.at[index], partner)
        yield
        swap.wait()
        for piece in range(dp):
            for line in range(2):
                summed = terms[index, piece, lines_of(core, line)] + swap_in[index, piece, line].astype(jnp.float32)
                wide[index, piece, line] = summed
                narrow[index, piece, line] = summed.astype(jnp.bfloat16)
        copies = [
            send_to(narrow.at[index, places[0], places[1]], plane_in.at[index, i], {"dp": places[0], "height": places[1]})
            for i, places in enumerate(plane_peers)
        ]
        yield
        wait_all(copies)
        summed = wide[index, clip, half]
        for i in range(len(plane_peers)):
            summed = summed + plane_in[index, i].astype(jnp.float32)
        for block in range(depth):
            start, stop = block * width, min((block + 1) * width, summed.shape[1])
            if start < stop:
                value = summed[:, start:stop]
                wide_z[index, block, :, : stop - start] = value
                narrow_z[index, block, :, : stop - start] = value.astype(jnp.bfloat16)
        copies = [
            send_to(narrow_z.at[index, peer], got_z.at[index, i], {"tm": peer * 2 + core})
            for i, peer in enumerate(level_peers)
        ]
        yield
        wait_all(copies)
        summed = wide_z[index, level]
        for i in range(depth - 1):
            summed = summed + got_z[index, i].astype(jnp.float32)
        mine[index, core, half, level] = summed.astype(jnp.bfloat16)
        own = mine.at[index, core, half, level]
        along = [send_to(own, own, {"tm": peer * 2 + core}) for peer in level_peers]
        across, inside = [], []

        def pass_on(owner, step, targets):
            block = mine.at[index, core, owner, (level + depth - step) % depth]
            for copies, place in targets:
                copies.append(send_to(block, block, place))

        both = ((across, {"height": other}), (inside, partner))
        pass_on(half, 0, both)
        yield
        for step in range(1, depth):
            along[step - 1].wait()
            pass_on(half, step, both)
        yield
        for step in range(depth):
            across[step].wait()
            pass_on(other, step, both[1:])
        yield
        wait_all(inside)
        for place in range(2):
            for line in range(2):
                top = place * share + line * band
                for block in range(depth):
                    start, stop = block * width, min((block + 1) * width, chunk)
                    if start < stop:
                        value = mine[index, place, line, block].astype(jnp.float32) * scale
                        grad_own[index, top : top + band, start:stop] = value[:, : stop - start]
        copies_out.append(bring(grad_own.at[index], (grad_one, grad_two)[index]))

    copies_out = []

    def finish_branch(frame, row, value):
        block_own[frame, row] = x_own[frame, row].astype(jnp.float32) + value
        if row == rows - 1:
            copies_out.append(bring(block_own.at[frame], block_out.at[frame]))

    def finish_input(frame, row, value):
        back = act_back(x_own[frame, row].astype(jnp.float32), value)
        input_own[frame, row] = cot_own[frame + 2, row].astype(jnp.float32) + back
        if row == rows - 1:
            copies_out.append(bring(input_own.at[frame], input_out.at[frame]))

    kernel_grad(0, acts_one, middle_grad)
    first = reduce(0)
    next(first)
    act_rows()
    fill_rows(acts_two, 2, False, same)
    act_time()
    fill_time(acts_two, 2, False, same)
    kernel_grad(1, acts_two, cot_own)
    next(first)
    second = reduce(1)
    next(second)
    steps = conv(acts_two, ahead_weights[1], range(frames + 2), finish_branch)
    run(steps[:3])
    next(second)
    run(steps[3:])
    grad_rows()
    fill_rows(grads_one, 3, True, same)
    grad_time()
    fill_time(grads_one, 3, True, same)
    next(first)
    steps = conv(grads_one, back_weights[0], range(frames + 2), finish_input)
    run(steps[:3])
    next(second)
    run(steps[3:])
    going = [first, second]
    while going:
        for task in list(going):
            if next(task, 0) == 0:
                going.remove(task)
    wait_all(copies_out)


def deliver(*refs):
    count = len(refs) // 2
    copies = [pltpu.make_async_copy(refs[i], refs[count + i], refs[-1].at[i]) for i in range(count)]
    for copy in copies:
        copy.start()
    for copy in copies:
        copy.wait()


def local(clip_input, cotangent, first_kernel, second_kernel):
    dp, heights, depth = (lax.axis_size("dp"), lax.axis_size("height"), lax.axis_size("tm") // 2)
    assert heights == 2
    _, frames, rows, channels, cols = clip_input.shape
    taps = first_kernel.shape[0]
    chunk = taps // dp
    band = channels // 4
    width = -(-chunk // (cols * depth)) * cols
    lanes = -(-chunk // cols) * cols
    sends = 2 * (1 + (2 * dp - 1) + 2 * (depth - 1) + 3 * depth)
    tile = (channels, cols)
    own = (frames, rows) + tile
    block = (depth, band, width)
    anywhere = pl.BlockSpec(memory_space=pl.ANY)
    field = pltpu.VMEM((frames + 2, rows + 2, 3 * channels, cols), jnp.bfloat16)
    padded = pltpu.VMEM((frames + 4, rows) + tile, jnp.bfloat16)
    weights = pltpu.VMEM((2, 3 * channels, 9 * channels), jnp.bfloat16)
    positions = frames * rows * cols * dp * heights * lax.axis_size("tm")
    found = pl.pallas_call(
        functools.partial(body, (dp, heights, depth), 1.0 / math.sqrt(positions)),
        out_shape=(
            jax.ShapeDtypeStruct(own, jnp.float32),
            jax.ShapeDtypeStruct(own, jnp.float32),
            jax.ShapeDtypeStruct((channels, chunk), jnp.float32),
            jax.ShapeDtypeStruct((channels, chunk), jnp.float32),
        ),
        in_specs=[pl.BlockSpec(memory_space=pltpu.HBM)] * 4,
        out_specs=(anywhere,) * 4,
        scratch_shapes=[
            pltpu.VMEM(own, jnp.bfloat16),
            padded,
            pltpu.VMEM((2, channels, taps), jnp.bfloat16),
            weights,
            weights,
            field,
            field,
            field,
            field,
            pltpu.VMEM(own, jnp.float32),
            pltpu.VMEM(own, jnp.bfloat16),
            padded,
            pltpu.VMEM(own, jnp.float32),
            pltpu.VMEM(own, jnp.float32),
            pltpu.VMEM(own, jnp.float32),
            pltpu.VMEM((2, channels, chunk), jnp.float32),
            pltpu.VMEM((4, 2, rows) + tile, jnp.bfloat16),
            pltpu.VMEM((4, frames) + tile, jnp.bfloat16),
            pltpu.VMEM((4, 2) + tile, jnp.bfloat16),
            pltpu.VMEM((2, dp, channels, lanes), jnp.float32),
            pltpu.VMEM((2, dp, 2, band, lanes), jnp.bfloat16),
            pltpu.VMEM((2, dp, 2, band, lanes), jnp.bfloat16),
            pltpu.VMEM((2, dp, 2, band, lanes), jnp.float32),
            pltpu.VMEM((2, dp, 2, band, lanes), jnp.bfloat16),
            pltpu.VMEM((2, 2 * dp - 1, band, lanes), jnp.bfloat16),
            pltpu.VMEM((2,) + block, jnp.float32),
            pltpu.VMEM((2,) + block, jnp.bfloat16),
            pltpu.VMEM((2, depth - 1, band, width), jnp.bfloat16),
            pltpu.VMEM((2, 2, 2) + block, jnp.bfloat16),
            pltpu.SemaphoreType.DMA((4, 3)),
            pltpu.SemaphoreType.DMA((4, 3)),
            pltpu.SemaphoreType.DMA((sends,)),
            pltpu.SemaphoreType.DMA((sends,)),
            pltpu.SemaphoreType.DMA((6 + 2 * frames,)),
        ],
        compiler_params=pltpu.CompilerParams(
            collective_id=0, has_side_effects=True, vmem_limit_bytes=VMEM_BYTES
        ),
        name="block_step",
    )(*[pltpu.with_memory_space_constraint(value, pltpu.HBM) for value in (clip_input[0], cotangent[0], first_kernel.T, second_kernel.T)])
    block_output, input_grad, grad_one, grad_two = pl.pallas_call(
        deliver,
        out_shape=[jax.ShapeDtypeStruct(value.shape, value.dtype) for value in found],
        in_specs=[anywhere] * len(found),
        out_specs=[anywhere] * len(found),
        scratch_shapes=[pltpu.SemaphoreType.DMA((len(found),))],
        compiler_params=pltpu.CompilerParams(vmem_limit_bytes=1 << 20),
        name="deliver",
    )(*found)
    return (block_output[None], input_grad[None], grad_one.T, grad_two.T)


def solution(mesh):
    split = P("dp", "tm", "height", None, None)
    return jax.shard_map(
        local,
        mesh=mesh,
        in_specs=(split, split, P(), P()),
        out_specs=(split, split, P("dp", None), P("dp", None)),
        check_vma=False,
    )
```

```python
import functools
import math

import jax
import jax.numpy as jnp
from jax import lax
from jax.experimental import pallas as pl
from jax.experimental.pallas import tpu as pltpu
from jax.sharding import PartitionSpec as P

EPSILON = 1e-06
MESH_IDS = pl.DeviceIdType.MESH
VMEM_BYTES = 40 << 20


def factor_of(value):
    return lax.rsqrt(jnp.mean(value * value, axis=0, keepdims=True) + EPSILON)


def act(value):
    scaled = value * factor_of(value)
    return scaled / (1.0 + jnp.exp(-scaled))


def act_back(value, grad):
    factor = factor_of(value)
    scaled = value * factor
    gate = 1.0 / (1.0 + jnp.exp(-scaled))
    inner = grad * (gate * (1.0 + scaled * (1.0 - gate)))
    return factor * (inner - scaled * jnp.mean(inner * scaled, axis=0, keepdims=True))


def body(
    sizes,
    scale,
    x,
    cot,
    turned_one,
    turned_two,
    block_out,
    input_out,
    grad_one,
    grad_two,
    x_own,
    cot_own,
    turned,
    ahead_weights,
    back_weights,
    acts_one,
    acts_two,
    grads_two,
    grads_one,
    middle,
    second_act,
    middle_grad,
    partial,
    block_own,
    input_own,
    grad_own,
    time_halo,
    row_halo,
    corner_halo,
    terms,
    swap_out,
    swap_in,
    wide,
    narrow,
    plane_in,
    wide_z,
    narrow_z,
    got_z,
    mine,
    halo_send,
    halo_recv,
    send,
    recv,
    local_sem,
):
    dp, heights, depth = sizes
    frames, rows, channels, cols = x.shape
    shards = 2 * depth
    chunk = grad_one.shape[1]
    band, width = narrow_z.shape[2:]
    shard = lax.axis_index("tm")
    core, level = shard % 2, shard // 2
    clip, half = lax.axis_index("dp"), lax.axis_index("height")
    other = 1 - half
    has_before, has_after = shard > 0, shard < shards - 1
    edge_row = (rows - 1) * other
    halo_row = (rows + 1) * other
    rim_row = (rows + 1) * half

    barrier = pltpu.get_barrier_semaphore()
    partner = {"tm": level * 2 + 1 - core}
    clip_peers = [(clip + step) % dp for step in range(1, dp)]
    level_peers = [(level + step) % depth for step in range(1, depth)]
    places = [partner, {"height": other}]
    places += [{"dp": peer} for peer in clip_peers]
    places += [{"tm": peer * 2 + core} for peer in level_peers]

    plane_peers = [(peer, owner) for owner in (half, other) for peer in clip_peers] + [(clip, other)]
    places += [{"dp": peer, "height": other} for peer in clip_peers]

    def greet(place):
        pl.semaphore_signal(barrier, inc=1, device_id=place, device_id_type=MESH_IDS)

    for place in places:
        greet(place)

    outer = shard + 2 * core - 1
    has_outer = jnp.logical_and(outer >= 0, outer < shards)

    @pl.when(has_outer)
    def _():
        greet({"tm": outer})

    @pl.when(has_before)
    def _():
        greet({"tm": shard - 1, "height": other})

    @pl.when(has_after)
    def _():
        greet({"tm": shard + 1, "height": other})

    taken = [0]

    def bring(source, target):
        copy = pltpu.make_async_copy(source, target, local_sem.at[taken[0]])
        taken[0] += 1
        copy.start()
        return copy

    inner = pl.ds(2, frames)
    weights_come = [bring(turned_one, turned.at[0]), bring(turned_two, turned.at[1])]
    x_comes = bring(x, x_own)
    cot_comes = bring(cot, cot_own.at[inner])

    near = has_outer.astype(jnp.int32) + has_before.astype(jnp.int32) + has_after.astype(jnp.int32)
    pl.semaphore_wait(barrier, len(places) + near)

    def remote(source, target, sender, receiver, place):
        return pltpu.make_async_remote_copy(
            src_ref=source,
            dst_ref=target,
            send_sem=sender,
            recv_sem=receiver,
            device_id=place,
            device_id_type=MESH_IDS,
        )

    def exchange(own, slot, ahead):
        step = -1 if ahead else 1
        start = 0 if ahead else frames - 2
        goes, comes = (has_before, has_after) if ahead else (has_after, has_before)
        span = pl.ds(start, 2)
        along = remote(own.at[span], time_halo.at[slot], halo_send.at[slot, 0], halo_recv.at[slot, 0], {"tm": shard + step})
        across = remote(own.at[:, edge_row], row_halo.at[slot], halo_send.at[slot, 1], halo_recv.at[slot, 1], {"height": other})
        corner = remote(
            own.at[span, edge_row],
            corner_halo.at[slot],
            halo_send.at[slot, 2],
            halo_recv.at[slot, 2],
            {"tm": shard + step, "height": other},
        )

        def send_time():
            @pl.when(goes)
            def _():
                along.start()
                corner.start()

        def wait_time():
            @pl.when(goes)
            def _():
                along.wait_send()
                corner.wait_send()

            @pl.when(comes)
            def _():
                along.wait_recv()
                corner.wait_recv()

        return across.start, send_time, across.wait, wait_time

    x_rows_go, x_time_goes, x_rows, x_time = exchange(x, 0, False)
    cot_rows_go, cot_time_goes, cot_rows, cot_time = exchange(cot, 1, True)
    x_rows_go()
    x_time_goes()

    lane = lax.broadcasted_iota(jnp.int32, (channels, cols), 1)

    def place_tile(field, frame, row, value):
        wide_value = value.astype(jnp.float32)
        left = jnp.where(lane == 0, 0.0, pltpu.roll(wide_value, 1, axis=1))
        right = jnp.where(lane == cols - 1, 0.0, pltpu.roll(wide_value, cols - 1, axis=1))
        field[frame, row, 0:channels] = left.astype(jnp.bfloat16)
        field[frame, row, channels : 2 * channels] = value
        field[frame, row, 2 * channels : 3 * channels] = right.astype(jnp.bfloat16)

    def clear(field, ahead):
        outside = frames if ahead else 0
        blank = jnp.zeros((3 * channels, cols), jnp.bfloat16)
        for frame in range(frames + 2):
            field[frame, rim_row] = blank
        for frame in range(outside, outside + 2):
            for row in range(rows + 2):
                field[frame, row] = blank

    def fill_rows(field, slot, ahead, make):
        inside = 0 if ahead else 2
        for frame in range(frames):
            place_tile(field, inside + frame, halo_row, make(row_halo[slot, frame]))

    def fill_time(field, slot, ahead, make):
        outside = frames if ahead else 0

        @pl.when(has_after if ahead else has_before)
        def _():
            def step(frame, carry):
                for row in range(rows):
                    place_tile(field, outside + frame, row + 1, make(time_halo[slot, frame, row]))
                place_tile(field, outside + frame, halo_row, make(corner_halo[slot, frame]))
                return carry

            lax.fori_loop(0, 2, step, 0)

    def conv(field, weights, order, finish):
        seen = [0] * frames

        def step(frame):
            taps = [tap for tap in range(3) if 0 <= frame - tap < frames]
            least = taps[0]
            patch = jnp.concatenate([field[frame, row : row + 3].reshape(9 * channels, cols) for row in range(rows)], axis=1)
            lines = weights[least * channels : (taps[-1] + 1) * channels]
            part = jnp.dot(lines, patch, preferred_element_type=jnp.float32)
            for tap in taps:
                target = frame - tap
                seen[target] += 1
                for row in range(rows):
                    value = part[(tap - least) * channels : (tap - least + 1) * channels, row * cols : (row + 1) * cols]
                    if seen[target] > 1:
                        value = partial[target, row] + value
                    if seen[target] == 3:
                        finish(target, row, value)
                    else:
                        partial[target, row] = value

        return [functools.partial(step, frame) for frame in order]

    def run(steps):
        for step in steps:
            step()

    def kernel_grad(slot, field, grad):
        tiles = [(frame, row) for frame in range(frames + 2) for row in range(rows)]
        left = jnp.concatenate(
            [jnp.concatenate([grad[frame - tap + 2, row] for frame, row in tiles], axis=1) for tap in range(3)], axis=0
        )
        right = jnp.concatenate([field[frame, row : row + 3].reshape(9 * channels, cols) for frame, row in tiles], axis=1)
        found = lax.dot_general(left, right, (((1,), (1,)), ((), ())), preferred_element_type=jnp.float32)
        span = 9 * channels
        for tap in range(3):
            for piece in range(dp):
                start, stop = max(tap * span, piece * chunk), min((tap + 1) * span, (piece + 1) * chunk)
                if start < stop:
                    value = found[tap * channels : (tap + 1) * channels, start - tap * span : stop - tap * span]
                    terms[slot, piece, :, start - piece * chunk : stop - piece * chunk] = value

    def as_act(value):
        return act(value.astype(jnp.float32)).astype(jnp.bfloat16)

    def same(value):
        return value

    for field, ahead in ((acts_one, False), (acts_two, False), (grads_two, True), (grads_one, True)):
        clear(field, ahead)
    blank_tile = jnp.zeros((channels, cols), jnp.bfloat16)
    for padded in (cot_own, middle_grad):
        for frame in (0, 1, frames + 2, frames + 3):
            for row in range(rows):
                padded[frame, row] = blank_tile

    x_comes.wait()

    def own_acts(frame, carry):
        for row in range(rows):
            place_tile(acts_one, frame + 2, row + 1, as_act(x_own[frame, row]))
        return carry

    lax.fori_loop(0, frames, own_acts, 0)
    for index, copy in enumerate(weights_come):
        copy.wait()
        plain = jnp.transpose(turned[index])
        for tap in range(3):
            lines = slice(tap * channels, (tap + 1) * channels)
            ahead_weights[index, lines] = turned[index, :, tap * 9 * channels : (tap + 1) * 9 * channels]
            last = 26 - 9 * tap
            tiles = [plain[(last - place) * channels : (last - place + 1) * channels] for place in range(9)]
            back_weights[index, lines] = jnp.concatenate(tiles, axis=1)
    cot_comes.wait()

    def own_grads(frame, carry):
        for row in range(rows):
            place_tile(grads_two, frame, row + 1, cot_own[frame + 2, row])
        return carry

    lax.fori_loop(0, frames, own_grads, 0)

    def finish_middle(frame, row, value):
        middle[frame, row] = value
        rounded = act(value).astype(jnp.bfloat16)
        second_act[frame, row] = rounded
        place_tile(acts_two, frame + 2, row + 1, rounded)

    act_rows_go, act_time_goes, act_rows, act_time = exchange(second_act, 2, False)
    cot_rows_go()
    cot_time_goes()
    x_rows()
    fill_rows(acts_one, 0, False, as_act)
    steps = conv(acts_one, ahead_weights[0], range(frames + 1, -1, -1), finish_middle)
    run(steps[:frames])
    act_time_goes()
    x_time()
    fill_time(acts_one, 0, False, as_act)
    run(steps[frames:])
    act_rows_go()

    def finish_back(frame, row, value):
        rounded = act_back(middle[frame, row], value).astype(jnp.bfloat16)
        middle_grad[frame + 2, row] = rounded
        place_tile(grads_one, frame, row + 1, rounded)

    grad_rows_go, grad_time_goes, grad_rows, grad_time = exchange(middle_grad.at[inner], 3, True)
    cot_rows()
    fill_rows(grads_two, 1, True, same)
    steps = conv(grads_two, back_weights[1], range(frames + 2), finish_back)
    run(steps[:frames])
    grad_time_goes()
    cot_time()
    fill_time(grads_two, 1, True, same)
    run(steps[frames:])
    grad_rows_go()

    used = [0]

    def send_to(source, target, place):
        slot = used[0]
        used[0] += 1
        copy = remote(source, target, send.at[slot], recv.at[slot], place)
        copy.start()
        return copy

    def wait_all(copies):
        for copy in copies:
            copy.wait()

    def reduce(index):
        share = channels // 2

        def lines_of(owner, line):
            return pl.ds(pl.multiple_of(owner * share + line * band, band), band)

        for piece in range(dp):
            for line in range(2):
                swap_out[index, piece, line] = terms[index, piece, lines_of(1 - core, line)].astype(jnp.bfloat16)
        swap = send_to(swap_out.at[index], swap_in.at[index], partner)
        yield
        swap.wait()
        for piece in range(dp):
            for line in range(2):
                summed = terms[index, piece, lines_of(core, line)] + swap_in[index, piece, line].astype(jnp.float32)
                wide[index, piece, line] = summed
                narrow[index, piece, line] = summed.astype(jnp.bfloat16)
        copies = [
            send_to(narrow.at[index, places[0], places[1]], plane_in.at[index, i], {"dp": places[0], "height": places[1]})
            for i, places in enumerate(plane_peers)
        ]
        yield
        wait_all(copies)
        summed = wide[index, clip, half]
        for i in range(len(plane_peers)):
            summed = summed + plane_in[index, i].astype(jnp.float32)
        for block in range(depth):
            start, stop = block * width, min((block + 1) * width, summed.shape[1])
            if start < stop:
                value = summed[:, start:stop]
                wide_z[index, block, :, : stop - start] = value
                narrow_z[index, block, :, : stop - start] = value.astype(jnp.bfloat16)
        copies = [
            send_to(narrow_z.at[index, peer], got_z.at[index, i], {"tm": peer * 2 + core})
            for i, peer in enumerate(level_peers)
        ]
        yield
        wait_all(copies)
        summed = wide_z[index, level]
        for i in range(depth - 1):
            summed = summed + got_z[index, i].astype(jnp.float32)
        mine[index, core, half, level] = summed.astype(jnp.bfloat16)
        own = mine.at[index, core, half, level]
        along = [send_to(own, own, {"tm": peer * 2 + core}) for peer in level_peers]
        across, inside = [], []

        def pass_on(owner, step, targets):
            block = mine.at[index, core, owner, (level + depth - step) % depth]
            for copies, place in targets:
                copies.append(send_to(block, block, place))

        def pass_inside(owner):
            region = mine.at[index, core, owner]
            inside.append(send_to(region, region, partner))

        both = ((across, {"height": other}),)
        pass_on(half, 0, both)
        yield
        for step in range(1, depth):
            along[step - 1].wait()
            pass_on(half, step, both)
        pass_inside(half)
        yield
        wait_all(across)
        pass_inside(other)
        yield
        wait_all(inside)
        for place in range(2):
            for line in range(2):
                top = place * share + line * band
                for block in range(depth):
                    start, stop = block * width, min((block + 1) * width, chunk)
                    if start < stop:
                        value = mine[index, place, line, block].astype(jnp.float32) * scale
                        grad_own[index, top : top + band, start:stop] = value[:, : stop - start]
        copies_out.append(bring(grad_own.at[index], (grad_one, grad_two)[index]))

    copies_out = []

    def finish_branch(frame, row, value):
        block_own[frame, row] = x_own[frame, row].astype(jnp.float32) + value
        if row == rows - 1:
            copies_out.append(bring(block_own.at[frame], block_out.at[frame]))

    def finish_input(frame, row, value):
        back = act_back(x_own[frame, row].astype(jnp.float32), value)
        input_own[frame, row] = cot_own[frame + 2, row].astype(jnp.float32) + back
        if row == rows - 1:
            copies_out.append(bring(input_own.at[frame], input_out.at[frame]))

    kernel_grad(0, acts_one, middle_grad)
    first = reduce(0)
    next(first)
    act_rows()
    fill_rows(acts_two, 2, False, same)
    act_time()
    fill_time(acts_two, 2, False, same)
    kernel_grad(1, acts_two, cot_own)
    next(first)
    second = reduce(1)
    next(second)
    steps = conv(acts_two, ahead_weights[1], range(frames + 2), finish_branch)
    run(steps[:3])
    next(second)
    run(steps[3:])
    grad_rows()
    fill_rows(grads_one, 3, True, same)
    grad_time()
    fill_time(grads_one, 3, True, same)
    next(first)
    steps = conv(grads_one, back_weights[0], range(frames + 2), finish_input)
    run(steps[:3])
    next(second)
    run(steps[3:])
    going = [first, second]
    while going:
        for task in list(going):
            if next(task, 0) == 0:
                going.remove(task)
    wait_all(copies_out)


def deliver(*refs):
    count = len(refs) // 2
    copies = [pltpu.make_async_copy(refs[i], refs[count + i], refs[-1].at[i]) for i in range(count)]
    for copy in copies:
        copy.start()
    for copy in copies:
        copy.wait()


def local(clip_input, cotangent, first_kernel, second_kernel):
    dp, heights, depth = (lax.axis_size("dp"), lax.axis_size("height"), lax.axis_size("tm") // 2)
    assert heights == 2
    _, frames, rows, channels, cols = clip_input.shape
    taps = first_kernel.shape[0]
    chunk = taps // dp
    band = channels // 4
    width = -(-chunk // (cols * depth)) * cols
    lanes = -(-chunk // cols) * cols
    sends = 2 * (1 + (2 * dp - 1) + 2 * (depth - 1) + 3 * depth)
    tile = (channels, cols)
    own = (frames, rows) + tile
    block = (depth, band, width)
    anywhere = pl.BlockSpec(memory_space=pl.ANY)
    field = pltpu.VMEM((frames + 2, rows + 2, 3 * channels, cols), jnp.bfloat16)
    padded = pltpu.VMEM((frames + 4, rows) + tile, jnp.bfloat16)
    weights = pltpu.VMEM((2, 3 * channels, 9 * channels), jnp.bfloat16)
    positions = frames * rows * cols * dp * heights * lax.axis_size("tm")
    found = pl.pallas_call(
        functools.partial(body, (dp, heights, depth), 1.0 / math.sqrt(positions)),
        out_shape=(
            jax.ShapeDtypeStruct(own, jnp.float32),
            jax.ShapeDtypeStruct(own, jnp.float32),
            jax.ShapeDtypeStruct((channels, chunk), jnp.float32),
            jax.ShapeDtypeStruct((channels, chunk), jnp.float32),
        ),
        in_specs=[pl.BlockSpec(memory_space=pltpu.HBM)] * 4,
        out_specs=(anywhere,) * 4,
        scratch_shapes=[
            pltpu.VMEM(own, jnp.bfloat16),
            padded,
            pltpu.VMEM((2, channels, taps), jnp.bfloat16),
            weights,
            weights,
            field,
            field,
            field,
            field,
            pltpu.VMEM(own, jnp.float32),
            pltpu.VMEM(own, jnp.bfloat16),
            padded,
            pltpu.VMEM(own, jnp.float32),
            pltpu.VMEM(own, jnp.float32),
            pltpu.VMEM(own, jnp.float32),
            pltpu.VMEM((2, channels, chunk), jnp.float32),
            pltpu.VMEM((4, 2, rows) + tile, jnp.bfloat16),
            pltpu.VMEM((4, frames) + tile, jnp.bfloat16),
            pltpu.VMEM((4, 2) + tile, jnp.bfloat16),
            pltpu.VMEM((2, dp, channels, lanes), jnp.float32),
            pltpu.VMEM((2, dp, 2, band, lanes), jnp.bfloat16),
            pltpu.VMEM((2, dp, 2, band, lanes), jnp.bfloat16),
            pltpu.VMEM((2, dp, 2, band, lanes), jnp.float32),
            pltpu.VMEM((2, dp, 2, band, lanes), jnp.bfloat16),
            pltpu.VMEM((2, 2 * dp - 1, band, lanes), jnp.bfloat16),
            pltpu.VMEM((2,) + block, jnp.float32),
            pltpu.VMEM((2,) + block, jnp.bfloat16),
            pltpu.VMEM((2, depth - 1, band, width), jnp.bfloat16),
            pltpu.VMEM((2, 2, 2) + block, jnp.bfloat16),
            pltpu.SemaphoreType.DMA((4, 3)),
            pltpu.SemaphoreType.DMA((4, 3)),
            pltpu.SemaphoreType.DMA((sends,)),
            pltpu.SemaphoreType.DMA((sends,)),
            pltpu.SemaphoreType.DMA((6 + 2 * frames,)),
        ],
        compiler_params=pltpu.CompilerParams(
            collective_id=0, has_side_effects=True, vmem_limit_bytes=VMEM_BYTES
        ),
        name="block_step",
    )(*[pltpu.with_memory_space_constraint(value, pltpu.HBM) for value in (clip_input[0], cotangent[0], first_kernel.T, second_kernel.T)])
    block_output, input_grad, grad_one, grad_two = pl.pallas_call(
        deliver,
        out_shape=[jax.ShapeDtypeStruct(value.shape, value.dtype) for value in found],
        in_specs=[anywhere] * len(found),
        out_specs=[anywhere] * len(found),
        scratch_shapes=[pltpu.SemaphoreType.DMA((len(found),))],
        compiler_params=pltpu.CompilerParams(vmem_limit_bytes=1 << 20),
        name="deliver",
    )(*found)
    return (block_output[None], input_grad[None], grad_one.T, grad_two.T)


def solution(mesh):
    split = P("dp", "tm", "height", None, None)
    return jax.shard_map(
        local,
        mesh=mesh,
        in_specs=(split, split, P(), P()),
        out_specs=(split, split, P("dp", None), P("dp", None)),
        check_vma=False,
    )
```
